128 devices in a mesh: dp: 4 (over y_lo, core), expert: 32 (over z, x, y_hi).
Axes of the slice: x: 4, y: 4 (y_hi: 2, y_lo: 2; y = y_hi * 2 + y_lo), z: 4, core: 2. Of those that a mesh axis runs over, the one named last changes fastest.
Arguments:
- hidden: bfloat16 [2048, 4096], P(('dp', 'expert')), may hold values from -6 to 6
- expert_ids: int32 [2048, 8], P(('dp', 'expert')), may hold values from 0 to 31, all different within a row; in each aligned block of 16 rows (0 to 15, 16 to 31, ...) at most 4 rows name the same one
- router_scores: float32 [2048, 8], P(('dp', 'expert')), may hold values from 0.05 to 1
- partner: int32 [32], replicated, may hold values from 0 to 31, as said below
- w_gate: bfloat16 [32, 4096, 1536], P('expert', None, 'dp'), may hold values from -0.09375 to 0.09375
- w_up: bfloat16 [32, 4096, 1536], P('expert', None, 'dp'), may hold values from -0.09375 to 0.09375
- w_down: bfloat16 [32, 4096, 1536], P('expert', None, 'dp'), may hold values from -0.15625 to 0.15625
Outputs:
- mixed: bfloat16 [2048, 4096], P(('dp', 'expert'))
- moved_gate: bfloat16 [32, 4096, 1536], P('expert', None, 'dp')
- moved_up: bfloat16 [32, 4096, 1536], P('expert', None, 'dp')
- moved_down: bfloat16 [32, 4096, 1536], P('expert', None, 'dp')
The draws below stay inside these ranges and needn't reach their ends.
Inputs may be any that keep to these rules, and one draw needn't show every extreme that they name: `expert_ids`: within the 16 rows of one device no expert is named by more than 4 rows, a bound that some block reaches. partner pairs the slots: partner[partner[t]] = t and partner[t] != t.
All inputs are finite; a program needn't handle non-finite values.
Results may differ from the reference program's by a relative error of at most 0.0058.
Values may be sent and summed in bfloat16 or wider, within the bound.
No kernel may reach another device: no remote copies, remote signals or barrier semaphores. Data moves between devices by JAX's collectives and lax.ppermute only.
A program may use at most 128 MiB of HBM per device.

```python
import math
import jax
import jax.numpy as jnp
import numpy as np
from jax import lax

D = 4096
FF = 1536
TOPK = 8
ROWS_DEV = 16
EXPERTS = 32
CAP = 4
TOKENS = 2048
N_DP = 4
N_EXPERT = 32


def draw_partner(key, part):
    order = jax.random.permutation(key, EXPERTS).astype(jnp.int32)
    mates = order[jnp.arange(EXPERTS, dtype=jnp.int32) ^ 1]
    return jnp.zeros((EXPERTS,), jnp.int32).at[order].set(mates)


def level_of(stream_key, dims, shards, smallest, top_value):
    def one(axis_at, blocks):
        steps = jax.random.uniform(jax.random.fold_in(jax.random.fold_in(stream_key, 6), axis_at), (blocks,), jnp.float32, smallest / len(shards), top_value / len(shards))
        return jnp.repeat(jnp.exp(steps), dims[axis_at] // blocks).reshape((-1,) + (1,) * (len(dims) - axis_at - 1))

    factor_of = one(*shards[0])
    for cut in shards[1:]:
        factor_of = factor_of * one(*cut)
    return factor_of


def routed_block(rng, own, number, rows, amount, top, bound, skew):
    order = jax.random.permutation(rng, amount)
    heavy_load, ordinary = portions_of(amount, rows * top, bound, skew, True), portions_of(amount, rows * top, bound, skew, False)
    places = jnp.arange(amount)

    def named(lengths, turn):
        used = int((lengths > 0).sum())
        fixed = max(1, used // 4)
        passed = fixed + (places - fixed + turn * (used - fixed)) % max(1, amount - fixed)
        return jnp.zeros((amount,), jnp.int32).at[order[jnp.where(places < fixed, places, passed)]].set(jnp.asarray(lengths, jnp.int32))

    lengths = jnp.where(number % 4 == 0, named(heavy_load, number // 4), named(ordinary, number - number // 4 - 1))
    mixed = jax.random.permutation(jax.random.fold_in(own, 3), amount)
    donor, taker = mixed[0:amount // 2 * 2:2], mixed[1:amount // 2 * 2:2]
    room = jnp.minimum(lengths[donor] - 1, bound - lengths[taker]) // 2
    room = jnp.where((donor == order[0]) | (taker == order[0]) | (lengths[taker] == 0), 0, jnp.maximum(room, 0))
    passed = jax.random.randint(jax.random.fold_in(own, 4), (amount // 2,), 0, 1 << 20) % (room + 1)
    lengths = lengths.at[donor].add(-passed).at[taker].add(passed)
    labels = jnp.searchsorted(jnp.cumsum(lengths), jnp.arange(rows * top), side="right").astype(jnp.int32)
    listing = labels.reshape(top, rows).T
    listing = listing[jax.random.permutation(jax.random.fold_in(own, 1), rows)]
    turn = jax.random.randint(jax.random.fold_in(own, 2), (rows, 1), 0, top)
    return jnp.take_along_axis(listing, (jnp.arange(top)[None, :] + turn) % top, axis=1)


def portions_of(number_of, total, limit, lean, full):
    weights = [(1 << 20) // math.isqrt(grade ** lean) + 1 for grade in range(1, number_of + 1)]
    largest = limit if full else min(limit, max(-(-total // number_of), total * weights[0] // sum(weights)))
    least = 1 if total - largest >= number_of - 1 else 0
    holding, surplus = [largest] + [least] * (number_of - 1), total - largest - least * (number_of - 1)
    while surplus > 0:
        candidates = [i for i in range(1, number_of) if holding[i] < largest] or [i for i in range(1, number_of) if holding[i] < limit]
        mass, remaining = sum([weights[i] for i in candidates]), surplus
        for i in candidates:
            addition = min(limit - holding[i], max(1, remaining * weights[i] // mass), surplus)
            holding[i] = holding[i] + addition
            surplus = surplus - addition
    return np.array(holding)


def gaussian(rng, dims, width, limit, pieces=(), kind=jnp.bfloat16):
    entries = width * jax.random.normal(rng, dims, jnp.float32)
    if pieces:
        entries = entries * level_of(rng, dims, pieces, -0.22, 0.18)
    return jnp.clip(entries, -limit, limit).astype(kind)


def setup_inputs(seed: int = 0) -> dict:
    keys = jax.random.split(jax.random.key(seed), 8)
    hidden = gaussian(keys[0], (TOKENS, D), 1.0, 6.0, ((0, 128),))
    expert_ids_keys = jax.random.split(jax.random.fold_in(keys[1], 1), TOKENS // ROWS_DEV)
    expert_ids_turns = jax.random.permutation(jax.random.fold_in(keys[1], 3), TOKENS // ROWS_DEV)
    expert_ids = jax.vmap(lambda own, number: routed_block(jax.random.fold_in(keys[1], 2), own, number, ROWS_DEV, EXPERTS, TOPK, CAP, 1))(expert_ids_keys, expert_ids_turns).reshape((TOKENS, TOPK))
    router_scores = jnp.clip(jnp.exp(math.log(1.0) - 2.9957323 * jax.random.uniform(keys[2], (TOKENS, TOPK), jnp.float32) ** level_of(keys[2], (TOKENS, TOPK), ((0, 128),), -0.2, 0.2)), 0.05, 1.0)
    partner = draw_partner(jax.random.fold_in(keys[7], 71), 0)
    w_gate = gaussian(keys[4], (EXPERTS, D, FF), D ** -0.5, 0.09375, ((0, 32), (2, 4)))
    w_up = gaussian(keys[5], (EXPERTS, D, FF), D ** -0.5, 0.09375, ((0, 32), (2, 4)))
    w_down = gaussian(keys[6], (EXPERTS, D, FF), FF ** -0.5, 0.15625, ((0, 32), (2, 4)))
    return {"hidden": hidden, "expert_ids": expert_ids, "router_scores": router_scores, "partner": partner, "w_gate": w_gate, "w_up": w_up, "w_down": w_down}


def reference(hidden, expert_ids, router_scores, partner, w_gate, w_up, w_down):
    row_weights = router_scores / jnp.sum(router_scores, axis=1, keepdims=True)
    capacity = min(ROWS_DEV, ROWS_DEV * TOPK * 9 // (8 * EXPERTS))
    most_rows = min(TOKENS, N_DP * N_EXPERT * capacity)
    quarter = FF // N_DP

    def per_expert(total, index):
        chosen = expert_ids == index
        weight = jnp.sum(jnp.where(chosen, row_weights, jnp.float32(0.0)), axis=1)
        used = jnp.any(chosen, axis=1)
        count = jnp.sum(used.astype(jnp.int32))
        picked = jnp.nonzero(used, size=most_rows, fill_value=0)[0].astype(jnp.int32)
        valid = jnp.arange(most_rows, dtype=jnp.int32) < count
        rows = hidden[picked]
        gate = jnp.dot(rows, w_gate[index], preferred_element_type=jnp.float32)
        upper = jnp.dot(rows, w_up[index], preferred_element_type=jnp.float32)
        inner = (jax.nn.silu(gate) * upper).astype(jnp.bfloat16)
        inner_q = inner.astype(jnp.float32).reshape(most_rows, N_DP, quarter)
        down_q = w_down[index].astype(jnp.float32).reshape(D, N_DP, quarter)
        parts = jnp.einsum("mqf,dqf->qmd", inner_q, down_q).astype(jnp.bfloat16)
        parts = lax.optimization_barrier(parts).astype(jnp.float32)
        scale = jnp.where(valid, weight[picked], jnp.float32(0.0))
        output = jnp.sum(parts, axis=0) * scale[:, None]
        return total.at[picked].add(output), None

    start = jnp.zeros((TOKENS, D), jnp.float32)
    total, _ = lax.scan(per_expert, start, jnp.arange(EXPERTS, dtype=jnp.int32))
    mixed = total.astype(jnp.bfloat16)
    return (mixed, w_gate[partner], w_up[partner], w_down[partner])
```

```python
import jax
import jax.numpy as jnp
from jax import lax
from jax.sharding import PartitionSpec as P

NZ, NX, NY = 4, 4, 2
SLOTS = 8


def expert_perm(dz, dx, dy):
    pairs = []
    for i in range(NZ * NX * NY):
        z, x, y = i // (NX * NY), (i // NY) % NX, i % NY
        j = ((z + dz) % NZ) * NX * NY + ((x + dx) % NX) * NY + (y + dy) % NY
        pairs.append((i, j))
    return pairs


def along_z(part, step):
    return lax.ppermute(part, "expert", expert_perm(step, 0, 0))


def along_x(part, step):
    return lax.ppermute(part, "expert", expert_perm(0, step, 0))


def along_y(part):
    return lax.ppermute(part, "expert", expert_perm(0, 0, 1))


def other_core(part):
    return lax.ppermute(part, "dp", [(i, i ^ 1) for i in range(4)])


def other_chip(part):
    return lax.ppermute(part, "dp", [(i, i ^ 2) for i in range(4)])


def relocate(partner, w_gate, w_up, w_down):
    experts = partner.shape[0]
    width, hidden_units = w_gate.shape[1:]
    piece = width // experts
    stacked = jnp.stack(
        [w.reshape(experts, piece, hidden_units) for w in (w_gate, w_up, w_down)], axis=1
    )
    spread = lax.all_to_all(stacked, "expert", split_axis=0, concat_axis=0, tiled=True)
    routed = spread.at[partner].get(mode="promise_in_bounds")
    back = lax.all_to_all(routed, "expert", split_axis=0, concat_axis=0, tiled=True)
    return tuple(back[:, i].reshape(1, width, hidden_units) for i in range(3))


def dispatch(buffer):
    got = [buffer[0]] + [along_z(buffer[k], k) for k in range(1, NZ)]
    by_x = []
    for j in range(NX):
        message = jnp.stack([g[j] for g in got])
        by_x.append(message if j == 0 else along_x(message, j))
    every = jnp.stack(by_x)
    return every[:, :, 0], along_y(every[:, :, 1])


def give_back(own, other):
    every = jnp.stack([own, along_y(other)], axis=2)
    by_x = [every[0]] + [along_x(every[j], -j) for j in range(1, NX)]
    got = []
    for k in range(NZ):
        message = jnp.stack([b[k] for b in by_x])
        got.append(message if k == 0 else along_z(message, -k))
    return jnp.stack(got)


def ffn(rows, w_gate, w_up, w_down):
    gate = jnp.dot(rows, w_gate, preferred_element_type=jnp.float32)
    upper = jnp.dot(rows, w_up, preferred_element_type=jnp.float32)
    inner = (jax.nn.silu(gate) * upper).astype(jnp.bfloat16)
    return lax.dot_general(
        inner, w_down, (((1,), (1,)), ((), ())), preferred_element_type=jnp.float32
    )


def local(hidden, expert_ids, router_scores, partner, w_gate, w_up, w_down):
    rows_here, width = hidden.shape
    half = width // 2
    place = lax.axis_index("expert")
    z, x, y = place // (NX * NY), (place // NY) % NX, place % NY
    core = lax.axis_index("dp") % 2
    first = core == 0
    moved = relocate(partner, w_gate, w_up, w_down)

    row_weights = router_scores / jnp.sum(router_scores, axis=1, keepdims=True)
    facts = jnp.concatenate([expert_ids.astype(jnp.float32), row_weights], axis=1)
    facts_other = other_core(facts)
    low, high = hidden[:, :half], hidden[:, half:]
    mine = jnp.where(first, low, high)
    theirs = other_core(jnp.where(first, high, low))

    def in_order(a, b):
        return jnp.where(first, jnp.concatenate([a, b]), jnp.concatenate([b, a]))

    facts = in_order(facts, facts_other)
    rows = in_order(mine, theirs)
    choose = expert_ids.shape[1]
    ids = facts[:, :choose].astype(jnp.int32)
    weights = facts[:, choose:]
    relative = (
        ((ids // (NX * NY) - z) % NZ) * (NX * NY)
        + (((ids // NY) % NX - x) % NX) * NY
        + (ids % NY + y) % NY
    )
    experts = NZ * NX * NY
    hits = relative[:, :, None] == jnp.arange(experts, dtype=jnp.int32)
    named = jnp.any(hits, axis=1)
    row_weight = jnp.sum(jnp.where(hits, weights[:, :, None], jnp.float32(0.0)), axis=1)
    count = 2 * rows_here
    before = jnp.tril(jnp.ones((count, count), jnp.bfloat16), -1)
    rank = jnp.dot(before, named.astype(jnp.bfloat16), preferred_element_type=jnp.float32)
    taken = jnp.logical_and(
        named[:, :, None], rank[:, :, None] == jnp.arange(SLOTS, dtype=jnp.float32)
    )
    combining = jnp.where(taken, row_weight[:, :, None], jnp.float32(0.0)).reshape(count, -1)
    placing = taken.astype(jnp.bfloat16).reshape(count, -1)
    buffer = lax.dot_general(
        placing, rows, (((0,), (0,)), ((), ())), preferred_element_type=jnp.float32
    )
    buffer = buffer.astype(jnp.bfloat16).reshape(NZ, NX, NY, SLOTS, half)

    own, other = dispatch(buffer)
    here = jnp.concatenate([own.reshape(-1, half), other.reshape(-1, half)])
    both = jnp.concatenate([here, other_chip(here)])
    both_other = other_core(both)
    features = jnp.where(
        first,
        jnp.concatenate([both, both_other], axis=1),
        jnp.concatenate([both_other, both], axis=1),
    )
    output = ffn(features, w_gate[0], w_up[0], w_down[0])
    keep = jnp.where(first, output[:, :half], output[:, half:])
    send = jnp.where(first, output[:, half:], output[:, :half]).astype(jnp.bfloat16)
    summed = keep + other_core(send).astype(jnp.float32)
    block = here.shape[0]
    total = summed[:block] + other_chip(summed[block:].astype(jnp.bfloat16)).astype(jnp.float32)
    total = total.astype(jnp.bfloat16).reshape(2, NX, NZ, SLOTS, half)
    returned = give_back(total[0], total[1]).reshape(-1, half)
    mixed = jnp.dot(
        combining,
        returned.astype(jnp.float32),
        precision=lax.Precision.HIGHEST,
        preferred_element_type=jnp.float32,
    ).astype(jnp.bfloat16)
    mine = jnp.where(first, mixed[:rows_here], mixed[rows_here:])
    theirs = other_core(jnp.where(first, mixed[rows_here:], mixed[:rows_here]))
    mixed = jnp.where(
        first,
        jnp.concatenate([mine, theirs], axis=1),
        jnp.concatenate([theirs, mine], axis=1),
    )
    return (mixed,) + moved


def solution(mesh):
    rows = P(("dp", "expert"), None)
    weights = P("expert", None, "dp")
    return jax.shard_map(
        local,
        mesh=mesh,
        in_specs=(rows, rows, rows, P(), weights, weights, weights),
        out_specs=(rows, weights, weights, weights),
        check_vma=False,
    )
```

```python
import jax
import jax.numpy as jnp
from jax import lax
from jax.experimental import pallas as pl
from jax.experimental.pallas import tpu as pltpu
from jax.sharding import PartitionSpec as P

EXPERTS = 32
SLOTS = 8
LANES = 384


def other_core(part):
    return lax.ppermute(part, "dp", [(i, i ^ 1) for i in range(4)])


def exchange(part):
    return lax.all_to_all(part, "expert", split_axis=0, concat_axis=0, tiled=True)


def pack_rows(rows):
    blocks = -(-rows.shape[1] // LANES)
    padded = jnp.pad(rows, ((0, 0), (0, blocks * LANES - rows.shape[1])))
    return [
        padded[:, b * LANES : (b + 1) * LANES].reshape(EXPERTS, SLOTS, LANES)
        for b in range(blocks)
    ]


def unpack_rows(packed, half):
    blocks = packed.shape[1] // SLOTS
    pieces = [
        packed[:, b * SLOTS : (b + 1) * SLOTS].reshape(EXPERTS * SLOTS, LANES)
        for b in range(blocks)
    ]
    pieces[-1] = pieces[-1][:, : half - (blocks - 1) * LANES]
    return jnp.concatenate(pieces, axis=1)


GROUP = 4


def pick_kernel(count, partner_ref, *refs):
    out = refs[-1]
    for g in range(GROUP):
        at = 0
        for i in range(count):
            block = refs[g * count + i]
            out[g, at : at + block.shape[1], :] = block[0]
            at += block.shape[1]


def pick(partner, sources):
    piece = 128
    count = len(sources)
    specs, operands = [], []
    for g in range(GROUP):
        for array, block in sources:
            specs.append(
                pl.BlockSpec(
                    (1, piece, LANES),
                    lambda i, p, g=g, block=block: (p[i * GROUP + g], block, 0),
                )
            )
            operands.append(array)
    size = EXPERTS * count * piece * LANES * 2
    return pl.pallas_call(
        lambda *refs: pick_kernel(count, *refs),
        out_shape=jax.ShapeDtypeStruct((EXPERTS, count * piece, LANES), jnp.bfloat16),
        grid_spec=pltpu.PrefetchScalarGridSpec(
            num_scalar_prefetch=1,
            grid=(EXPERTS // GROUP,),
            in_specs=specs,
            out_specs=pl.BlockSpec((GROUP, count * piece, LANES), lambda i, p: (i, 0, 0)),
        ),
        cost_estimate=pl.CostEstimate(flops=0, bytes_accessed=2 * size, transcendentals=0),
        name="pick",
    )(partner, *operands)


def ffn_kernel(rows_ref, gate_ref, up_ref, down_ref, out_ref):
    half = rows_ref.shape[2]

    def product(w_ref):
        return jnp.dot(
            rows_ref[0], w_ref[:half, :], preferred_element_type=jnp.float32
        ) + jnp.dot(rows_ref[1], w_ref[half:, :], preferred_element_type=jnp.float32)

    gate = product(gate_ref)
    upper = product(up_ref)
    inner = (gate / (1.0 + jnp.exp(-gate)) * upper).astype(jnp.bfloat16)
    for c in range(2):
        out_ref[c] = lax.dot_general(
            inner,
            down_ref[c * half : (c + 1) * half, :],
            (((1,), (1,)), ((), ())),
            preferred_element_type=jnp.float32,
        ).astype(jnp.bfloat16)


def ffn(rows, w_gate, w_up, w_down):
    groups, count, half = rows.shape
    width, hidden_units = w_gate.shape
    whole = pl.BlockSpec((width, hidden_units), lambda i: (0, 0))
    block = pl.BlockSpec((2, count, half), lambda i: (i, 0, 0))
    flops = 2 * 3 * groups * count * half * hidden_units
    size = 2 * (2 * groups * count * half + 3 * width * hidden_units)
    return pl.pallas_call(
        ffn_kernel,
        out_shape=jax.ShapeDtypeStruct(rows.shape, jnp.bfloat16),
        grid=(groups // 2,),
        in_specs=[block, whole, whole, whole],
        out_specs=block,
        compiler_params=pltpu.CompilerParams(vmem_limit_bytes=48 * 2**20),
        cost_estimate=pl.CostEstimate(
            flops=flops, bytes_accessed=size, transcendentals=groups * count * hidden_units // 2
        ),
        name="ffn",
    )(rows, w_gate, w_up, w_down)


def local(hidden, expert_ids, router_scores, partner, w_gate, w_up, w_down):
    rows_here, width = hidden.shape
    half = width // 2
    piece = width // EXPERTS
    first = lax.axis_index("dp") % 2 == 0
    gate, upper, down = (w.reshape(EXPERTS, piece, LANES) for w in (w_gate, w_up, w_down))

    row_weights = router_scores / jnp.sum(router_scores, axis=1, keepdims=True)
    facts = jnp.concatenate([expert_ids.astype(jnp.float32), row_weights], axis=1)
    facts_other = other_core(facts)
    low, high = hidden[:, :half], hidden[:, half:]
    mine = jnp.where(first, low, high)
    theirs = other_core(jnp.where(first, high, low))

    def in_order(a, b):
        return jnp.where(first, jnp.concatenate([a, b]), jnp.concatenate([b, a]))

    facts = in_order(facts, facts_other)
    rows = in_order(mine, theirs)
    choose = expert_ids.shape[1]
    ids = facts[:, :choose].astype(jnp.int32)
    weights = facts[:, choose:]
    hits = ids[:, :, None] == jnp.arange(EXPERTS, dtype=jnp.int32)
    named = jnp.any(hits, axis=1)
    row_weight = jnp.sum(jnp.where(hits, weights[:, :, None], jnp.float32(0.0)), axis=1)
    count = 2 * rows_here
    before = jnp.tril(jnp.ones((count, count), jnp.bfloat16), -1)
    rank = jnp.dot(before, named.astype(jnp.bfloat16), preferred_element_type=jnp.float32)
    taken = jnp.logical_and(
        named[:, :, None], rank[:, :, None] == jnp.arange(SLOTS, dtype=jnp.float32)
    )
    combining = jnp.where(taken, row_weight[:, :, None], jnp.float32(0.0)).reshape(count, -1)
    placing = taken.astype(jnp.bfloat16).reshape(count, -1)
    buffer = lax.dot_general(
        placing, rows, (((0,), (0,)), ((), ())), preferred_element_type=jnp.float32
    ).astype(jnp.bfloat16)

    spread_a = exchange(jnp.concatenate([gate] + pack_rows(buffer), axis=1))
    outgoing_b = jnp.concatenate([upper, down], axis=1)
    spread_a, outgoing_b = lax.optimization_barrier((spread_a, outgoing_b))
    spread_b = exchange(outgoing_b)

    arrived = unpack_rows(spread_a[:, piece:], half)
    every = lax.all_gather(arrived, "dp", axis=0)
    output = ffn(every, w_gate[0], w_up[0], w_down[0])
    total = lax.psum_scatter(output, "dp", scatter_dimension=0)

    routed_a = pick(partner, [(spread_a, 0), (spread_b, 0)])
    back_a = exchange(routed_a)
    routed_b = jnp.concatenate([pick(partner, [(spread_b, 1)])] + pack_rows(total), axis=1)
    back_a, routed_b = lax.optimization_barrier((back_a, routed_b))
    back_b = exchange(routed_b)

    returned = unpack_rows(back_b[:, piece:], half)
    mixed = jnp.dot(
        combining,
        returned.astype(jnp.float32),
        precision=lax.Precision.HIGHEST,
        preferred_element_type=jnp.float32,
    ).astype(jnp.bfloat16)
    mine = jnp.where(first, mixed[:rows_here], mixed[rows_here:])
    theirs = other_core(jnp.where(first, mixed[rows_here:], mixed[:rows_here]))
    mixed = jnp.where(
        first,
        jnp.concatenate([mine, theirs], axis=1),
        jnp.concatenate([theirs, mine], axis=1),
    )
    moved = (back_a[:, :piece], back_a[:, piece:], back_b[:, :piece])
    return (mixed,) + tuple(m.reshape(w_gate.shape) for m in moved)


def solution(mesh):
    rows = P(("dp", "expert"), None)
    weights = P("expert", None, "dp")
    return jax.shard_map(
        local,
        mesh=mesh,
        in_specs=(rows, rows, rows, P(), weights, weights, weights),
        out_specs=(rows, weights, weights, weights),
        check_vma=False,
    )
```

```python
import jax
import jax.numpy as jnp
from jax import lax
from jax.experimental import pallas as pl
from jax.experimental.pallas import tpu as pltpu
from jax.sharding import Mesh, PartitionSpec as P

NZ, NX, NY = 4, 4, 2
EXPERTS = NZ * NX * NY
PLANE = NZ * NX
SLOTS = 8
CAPACITIES = (8, 10, 12, PLANE)


def other_core(part):
    return lax.ppermute(part, "core", [(0, 1), (1, 0)])


def other_plane(part):
    return lax.ppermute(part, "y_hi", [(0, 1), (1, 0)])


def by_expert(part):
    return lax.all_to_all(part, ("z", "x", "y_hi"), split_axis=0, concat_axis=0, tiled=True)


def by_place(part):
    return lax.all_to_all(part, ("x", "z"), split_axis=0, concat_axis=0, tiled=True)


def routes(partner):
    side = lax.axis_index("y_hi")
    place = jnp.arange(PLANE, dtype=jnp.int32)
    expert = (place % NZ) * (NX * NY) + (place // NZ) * NY

    def mates(plane):
        onehot = expert[:, None] + plane == jnp.arange(EXPERTS, dtype=jnp.int32)[None, :]
        return jnp.sum(jnp.where(onehot, partner[None, :], 0), axis=1)

    def crossing_before(crossing):
        earlier = place[None, :] < place[:, None]
        return jnp.sum(jnp.where(earlier, crossing[None, :].astype(jnp.int32), 0), axis=1)

    mine, theirs = mates(side), mates(1 - side)
    crossing = mine % NY != side
    rank = crossing_before(crossing)
    rank_there = crossing_before(theirs % NY == side)
    sent = jnp.sum(
        jnp.where(jnp.logical_and(crossing[None, :], rank[None, :] == place[:, None]), place, 0),
        axis=1,
    )
    source = (mine // NY % NX) * NZ + mine // (NX * NY)
    arrived = jnp.sum(
        jnp.where(source[:, None] == place[None, :], rank_there[None, :], 0), axis=1
    )
    kept_at = jnp.where(crossing, 0, source)
    got_at = jnp.where(crossing, arrived, 0)
    count = jnp.sum(crossing.astype(jnp.int32))
    level = sum((count > c).astype(jnp.int32) for c in CAPACITIES[:-1])
    return level, sent, jnp.stack([kept_at, got_at, crossing.astype(jnp.int32)])


GROUP = 2


def pick_kernel(at_ref, *refs):
    out = refs[-1]
    for g in range(GROUP):
        out[g] = refs[g][0]


def pick(at, blocks, count):
    shape = blocks.shape[1:]
    size = 2 * count * shape[0] * shape[1]

    def spec(g):
        return pl.BlockSpec((1,) + shape, lambda i, at_ref: (at_ref[i * GROUP + g], 0, 0))

    return pl.pallas_call(
        pick_kernel,
        out_shape=jax.ShapeDtypeStruct((count,) + shape, blocks.dtype),
        grid_spec=pltpu.PrefetchScalarGridSpec(
            num_scalar_prefetch=1,
            grid=(count // GROUP,),
            in_specs=[spec(g) for g in range(GROUP)],
            out_specs=pl.BlockSpec((GROUP,) + shape, lambda i, at_ref: (i, 0, 0)),
        ),
        cost_estimate=pl.CostEstimate(flops=0, bytes_accessed=2 * size, transcendentals=0),
        name="pick",
    )(at, *([blocks] * GROUP))


def merge_kernel(at_ref, *refs):
    out = refs[-1]
    for g in range(GROUP):
        crossing = at_ref[2, pl.program_id(0) * GROUP + g]

        @pl.when(crossing == 0)
        def _():
            out[g] = refs[2 * g][0]

        @pl.when(crossing != 0)
        def _():
            out[g] = refs[2 * g + 1][0]


def merge(at, kept, got):
    shape = kept.shape[1:]
    size = 2 * PLANE * shape[0] * shape[1]

    def spec(g, row):
        return pl.BlockSpec((1,) + shape, lambda i, at_ref: (at_ref[row, i * GROUP + g], 0, 0))

    return pl.pallas_call(
        merge_kernel,
        out_shape=jax.ShapeDtypeStruct((PLANE,) + shape, kept.dtype),
        grid_spec=pltpu.PrefetchScalarGridSpec(
            num_scalar_prefetch=1,
            grid=(PLANE // GROUP,),
            in_specs=[spec(g, row) for g in range(GROUP) for row in range(2)],
            out_specs=pl.BlockSpec((GROUP,) + shape, lambda i, at_ref: (i, 0, 0)),
        ),
        cost_estimate=pl.CostEstimate(flops=0, bytes_accessed=2 * size, transcendentals=0),
        name="merge",
    )(at, *([kept, got] * GROUP))


def exchange_beside(level, sent, at, spread, outgoing):
    def branch(capacity):
        def run(sent, at, spread, outgoing):
            incoming = by_place(outgoing)
            got = other_plane(pick(sent, spread, capacity))
            return incoming, merge(at, spread, got)

        return run

    return lax.switch(level, [branch(c) for c in CAPACITIES], sent, at, spread, outgoing)


def ffn_kernel(rows_ref, gate_ref, up_ref, down_ref, out_ref):
    half = rows_ref.shape[2]

    def product(w_ref):
        return jnp.dot(
            rows_ref[0], w_ref[:half, :], preferred_element_type=jnp.float32
        ) + jnp.dot(rows_ref[1], w_ref[half:, :], preferred_element_type=jnp.float32)

    gate = product(gate_ref)
    upper = product(up_ref)
    inner = (gate / (1.0 + jnp.exp(-gate)) * upper).astype(jnp.bfloat16)
    for c in range(2):
        out_ref[c] = lax.dot_general(
            inner,
            down_ref[c * half : (c + 1) * half, :],
            (((1,), (1,)), ((), ())),
            preferred_element_type=jnp.float32,
        ).astype(jnp.bfloat16)


def ffn(rows, w_gate, w_up, w_down):
    groups, count, half = rows.shape
    width, hidden_units = w_gate.shape
    whole = pl.BlockSpec((width, hidden_units), lambda i: (0, 0))
    block = pl.BlockSpec((2, count, half), lambda i: (i, 0, 0))
    flops = 2 * 3 * groups * count * half * hidden_units
    size = 2 * (2 * groups * count * half + 3 * width * hidden_units)
    return pl.pallas_call(
        ffn_kernel,
        out_shape=jax.ShapeDtypeStruct(rows.shape, jnp.bfloat16),
        grid=(groups // 2,),
        in_specs=[block, whole, whole, whole],
        out_specs=block,
        compiler_params=pltpu.CompilerParams(vmem_limit_bytes=48 * 2**20),
        cost_estimate=pl.CostEstimate(
            flops=flops, bytes_accessed=size, transcendentals=groups * count * hidden_units // 2
        ),
        name="ffn",
    )(rows, w_gate, w_up, w_down)


def local(hidden, expert_ids, router_scores, partner, w_gate, w_up, w_down):
    rows_here, width = hidden.shape
    half = width // 2
    piece = width // PLANE
    cut = piece // 2
    hidden_units = w_gate.shape[2]
    first = lax.axis_index("core") == 0
    gate, upper, down = (
        w.reshape(PLANE, piece, hidden_units) for w in (w_gate, w_up, w_down)
    )

    row_weights = router_scores / jnp.sum(router_scores, axis=1, keepdims=True)
    facts = jnp.concatenate([expert_ids.astype(jnp.float32), row_weights], axis=1)
    facts_other = other_core(facts)
    low, high = hidden[:, :half], hidden[:, half:]
    mine = jnp.where(first, low, high)
    theirs = other_core(jnp.where(first, high, low))

    def in_order(a, b):
        return jnp.where(first, jnp.concatenate([a, b]), jnp.concatenate([b, a]))

    facts = in_order(facts, facts_other)
    rows = in_order(mine, theirs)
    choose = expert_ids.shape[1]
    ids = facts[:, :choose].astype(jnp.int32)
    weights = facts[:, choose:]
    hits = ids[:, :, None] == jnp.arange(EXPERTS, dtype=jnp.int32)
    named = jnp.any(hits, axis=1)
    row_weight = jnp.sum(jnp.where(hits, weights[:, :, None], jnp.float32(0.0)), axis=1)
    count = 2 * rows_here
    before = jnp.tril(jnp.ones((count, count), jnp.bfloat16), -1)
    rank = jnp.dot(before, named.astype(jnp.bfloat16), preferred_element_type=jnp.float32)
    taken = jnp.logical_and(
        named[:, :, None], rank[:, :, None] == jnp.arange(SLOTS, dtype=jnp.float32)
    )
    combining = jnp.where(taken, row_weight[:, :, None], jnp.float32(0.0)).reshape(count, -1)
    placing = taken.astype(jnp.bfloat16).reshape(count, -1)
    buffer = lax.dot_general(
        placing, rows, (((0,), (0,)), ((), ())), preferred_element_type=jnp.float32
    ).astype(jnp.bfloat16)
    arrived = by_expert(buffer.reshape(EXPERTS, SLOTS, half)).reshape(-1, half)

    level, sent, at = routes(partner)
    outgoing_a = jnp.concatenate([gate, upper[:, :cut]], axis=1)
    outgoing_b = jnp.concatenate([upper[:, cut:], down], axis=1)
    arrived, outgoing_a, outgoing_b = lax.optimization_barrier((arrived, outgoing_a, outgoing_b))
    spread_a = by_place(outgoing_a)

    every = lax.all_gather(arrived, ("y_lo", "core"), axis=0)
    output = ffn(every, w_gate[0], w_up[0], w_down[0])
    spread_a, output, outgoing_b = lax.optimization_barrier((spread_a, output, outgoing_b))
    total = lax.psum_scatter(output, ("y_lo", "core"), scatter_dimension=0)

    spread_b, routed_a = exchange_beside(level, sent, at, spread_a, outgoing_b)
    back_a, routed_b = exchange_beside(level, sent, at, spread_b, routed_a)
    total, routed_b = lax.optimization_barrier((total, routed_b))
    returned = by_expert(total.reshape(EXPERTS, SLOTS, half)).reshape(-1, half)
    returned, routed_b = lax.optimization_barrier((returned, routed_b))
    back_b = by_place(routed_b)

    mixed = jnp.dot(
        combining,
        returned.astype(jnp.float32),
        precision=lax.Precision.HIGHEST,
        preferred_element_type=jnp.float32,
    ).astype(jnp.bfloat16)
    mine = jnp.where(first, mixed[:rows_here], mixed[rows_here:])
    theirs = other_core(jnp.where(first, mixed[rows_here:], mixed[:rows_here]))
    mixed = jnp.where(
        first,
        jnp.concatenate([mine, theirs], axis=1),
        jnp.concatenate([theirs, mine], axis=1),
    )
    moved = (
        back_a[:, :piece],
        jnp.concatenate([back_a[:, piece:], back_b[:, :cut]], axis=1),
        back_b[:, cut:],
    )
    return (mixed,) + tuple(m.reshape(w_gate.shape) for m in moved)


def solution(mesh):
    chips = Mesh(mesh.devices.reshape(2, 2, NZ, NX, NY), ("y_lo", "core", "z", "x", "y_hi"))
    dp, expert = ("y_lo", "core"), ("z", "x", "y_hi")
    rows = P(dp + expert, None)
    weights = P(expert, None, dp)
    return jax.shard_map(
        local,
        mesh=chips,
        in_specs=(rows, rows, rows, P(), weights, weights, weights),
        out_specs=(rows, weights, weights, weights),
        check_vma=False,
    )
```

```python
import jax
import jax.numpy as jnp
from jax import lax
from jax.experimental import pallas as pl
from jax.experimental.pallas import tpu as pltpu
from jax.sharding import Mesh, PartitionSpec as P

NZ, NX, NY = 4, 4, 2
EXPERTS = NZ * NX * NY
PLANE = NZ * NX
SLOTS = 8
CAPACITY, MORE = 8, (2, PLANE - 8)


def other_core(part):
    return lax.ppermute(part, "core", [(0, 1), (1, 0)])


def other_plane(part):
    return lax.ppermute(part, "y_hi", [(0, 1), (1, 0)])


def near_chip(part):
    return lax.ppermute(part, "y_lo", [(0, 1), (1, 0)])


def diagonal_chip(part):
    return lax.ppermute(part, ("y_lo", "y_hi"), [(i, 3 - i) for i in range(4)])


def by_place(part):
    return lax.all_to_all(part, ("x", "z"), split_axis=0, concat_axis=0, tiled=True)


def routes(partner):
    side = lax.axis_index("y_hi")
    place = jnp.arange(PLANE, dtype=jnp.int32)
    expert = (place % NZ) * (NX * NY) + (place // NZ) * NY

    def mates(plane):
        onehot = expert[:, None] + plane == jnp.arange(EXPERTS, dtype=jnp.int32)[None, :]
        return jnp.sum(jnp.where(onehot, partner[None, :], 0), axis=1)

    def crossing_before(crossing):
        earlier = place[None, :] < place[:, None]
        return jnp.sum(jnp.where(earlier, crossing[None, :].astype(jnp.int32), 0), axis=1)

    mine, theirs = mates(side), mates(1 - side)
    crossing = mine % NY != side
    rank = crossing_before(crossing)
    rank_there = crossing_before(theirs % NY == side)
    sent = jnp.sum(
        jnp.where(jnp.logical_and(crossing[None, :], rank[None, :] == place[:, None]), place, 0),
        axis=1,
    )
    source = (mine // NY % NX) * NZ + mine // (NX * NY)
    arrived = jnp.sum(
        jnp.where(source[:, None] == place[None, :], rank_there[None, :], 0), axis=1
    )
    crosses = crossing.astype(jnp.int32)
    where = crosses * (1 + (arrived >= CAPACITY))
    at = jnp.stack(
        [
            jnp.where(crossing, 0, source),
            jnp.where(where == 1, arrived, 0),
            jnp.where(where == 2, arrived - CAPACITY, 0),
            where,
        ]
    )
    count = jnp.sum(crosses)
    level = (count > CAPACITY).astype(jnp.int32) + (count > CAPACITY + MORE[0])
    return level, sent, at


def pick_kernel(at_ref, *refs):
    out = refs[-1]
    for g in range(len(refs) - 1):
        out[g] = refs[g][0]


def pick(at, blocks, count):
    shape = blocks.shape[1:]
    group = count // 2
    size = 2 * count * shape[0] * shape[1]

    def spec(g):
        return pl.BlockSpec((1,) + shape, lambda i, at_ref: (at_ref[i * group + g], 0, 0))

    return pl.pallas_call(
        pick_kernel,
        out_shape=jax.ShapeDtypeStruct((count,) + shape, blocks.dtype),
        grid_spec=pltpu.PrefetchScalarGridSpec(
            num_scalar_prefetch=1,
            grid=(count // group,),
            in_specs=[spec(g) for g in range(group)],
            out_specs=pl.BlockSpec((group,) + shape, lambda i, at_ref: (i, 0, 0)),
        ),
        cost_estimate=pl.CostEstimate(flops=0, bytes_accessed=2 * size, transcendentals=0),
        name="pick",
    )(at, *([blocks] * group))


GROUP = 4


def merge_kernel(at_ref, *refs):
    out = refs[-1]
    for g in range(GROUP):
        where = at_ref[3, pl.program_id(0) * GROUP + g]
        for row in range(3):

            @pl.when(where == row)
            def _():
                out[g] = refs[3 * g + row][0]


def merge(at, sources):
    shape = sources[0].shape[1:]
    size = 2 * PLANE * shape[0] * shape[1]

    def spec(g, row):
        return pl.BlockSpec((1,) + shape, lambda i, at_ref: (at_ref[row, i * GROUP + g], 0, 0))

    return pl.pallas_call(
        merge_kernel,
        out_shape=jax.ShapeDtypeStruct((PLANE,) + shape, sources[0].dtype),
        grid_spec=pltpu.PrefetchScalarGridSpec(
            num_scalar_prefetch=1,
            grid=(PLANE // GROUP,),
            in_specs=[spec(g, row) for g in range(GROUP) for row in range(3)],
            out_specs=pl.BlockSpec((GROUP,) + shape, lambda i, at_ref: (i, 0, 0)),
        ),
        cost_estimate=pl.CostEstimate(flops=0, bytes_accessed=2 * size, transcendentals=0),
        name="merge",
    )(at, *(list(sources) * GROUP))


def across(more, sent, at, spread, got):
    def none(sent, spread):
        return jnp.zeros((MORE[-1],) + spread.shape[1:], spread.dtype)

    def some(count):
        def run(sent, spread):
            late = other_plane(pick(sent[CAPACITY : CAPACITY + count], spread, count))
            return jnp.pad(late, ((0, MORE[-1] - count), (0, 0), (0, 0)))

        return run

    late = lax.switch(more, [none] + [some(count) for count in MORE], sent, spread)
    return merge(at, [spread, got, late])


def copy_kernel(in_ref, out_ref):
    out_ref[...] = in_ref[...]


def duplicate(value):
    steps = 8
    block = pl.BlockSpec((value.shape[0] // steps,) + value.shape[1:], lambda i: (i, 0, 0))
    return pl.pallas_call(
        copy_kernel,
        out_shape=jax.ShapeDtypeStruct(value.shape, value.dtype),
        grid=(steps,),
        in_specs=[block],
        out_specs=block,
        cost_estimate=pl.CostEstimate(
            flops=0, bytes_accessed=4 * value.size, transcendentals=0
        ),
        name="duplicate",
    )(value)


def after(done, value):
    return lax.optimization_barrier((done, value))


def ffn_kernel(core_ref, *refs):
    mine, theirs, (gate_ref, up_ref, down_ref, keep_ref, send_ref) = refs[:2], refs[2:4], refs[4:]
    half = keep_ref.shape[1]
    here = pl.ds(pl.multiple_of(core_ref[0] * half, half), half)
    there = pl.ds(pl.multiple_of((1 - core_ref[0]) * half, half), half)
    across = (((1,), (1,)), ((), ()))
    for i in range(2):

        def product(w_ref):
            return jnp.dot(
                mine[i][...], w_ref[here, :], preferred_element_type=jnp.float32
            ) + jnp.dot(theirs[i][...], w_ref[there, :], preferred_element_type=jnp.float32)

        gate = product(gate_ref)
        upper = product(up_ref)
        inner = (gate / (1.0 + jnp.exp(-gate)) * upper).astype(jnp.bfloat16)
        count = mine[i].shape[0]
        rows = pl.ds(i * count, count)
        keep_ref[rows, :] = lax.dot_general(
            inner, down_ref[here, :], across, preferred_element_type=jnp.float32
        )
        send_ref[rows, :] = lax.dot_general(
            inner, down_ref[there, :], across, preferred_element_type=jnp.float32
        ).astype(jnp.bfloat16)


def ffn(core, mine, theirs, w_gate, w_up, w_down):
    count, half = mine[0].shape
    width, hidden_units = w_gate.shape
    flops = 2 * 3 * 2 * count * width * hidden_units
    size = 2 * (2 * count * width + 3 * width * hidden_units) + 6 * 2 * count * half
    vmem = pl.BlockSpec(memory_space=pltpu.VMEM)
    return pl.pallas_call(
        ffn_kernel,
        out_shape=(
            jax.ShapeDtypeStruct((2 * count, half), jnp.float32),
            jax.ShapeDtypeStruct((2 * count, half), jnp.bfloat16),
        ),
        in_specs=[pl.BlockSpec(memory_space=pltpu.SMEM)] + [vmem] * 7,
        out_specs=(vmem, vmem),
        compiler_params=pltpu.CompilerParams(vmem_limit_bytes=48 * 2**20),
        cost_estimate=pl.CostEstimate(
            flops=flops, bytes_accessed=size, transcendentals=2 * count * hidden_units
        ),
        name="ffn",
    )(core, *mine, *theirs, w_gate, w_up, w_down)


def local(hidden, expert_ids, router_scores, partner, w_gate, w_up, w_down):
    rows_here, width = hidden.shape
    half = width // 2
    piece = width // PLANE
    hidden_units = w_gate.shape[2]
    first = lax.axis_index("core") == 0
    gate, upper, down = (
        w.reshape(PLANE, piece, hidden_units) for w in (w_gate, w_up, w_down)
    )

    facts = jnp.concatenate([expert_ids.astype(jnp.float32), router_scores], axis=1)
    facts_other = other_core(facts)
    low, high = hidden[:, :half], hidden[:, half:]
    mine = jnp.where(first, low, high)
    theirs = other_core(jnp.where(first, high, low))

    def in_order(a, b):
        return jnp.where(first, jnp.concatenate([a, b]), jnp.concatenate([b, a]))

    facts = in_order(facts, facts_other)
    rows = in_order(mine, theirs)
    choose = expert_ids.shape[1]
    ids = facts[:, :choose].astype(jnp.int32)
    scores = facts[:, choose:]
    weights = scores / jnp.sum(scores, axis=1, keepdims=True)
    side = lax.axis_index("y_hi")
    relative = (ids // NY % NX * NZ + ids // (NX * NY)) * NY + (ids % NY != side)
    hits = relative[:, :, None] == jnp.arange(EXPERTS, dtype=jnp.int32)
    named = jnp.any(hits, axis=1)
    row_weight = jnp.sum(jnp.where(hits, weights[:, :, None], jnp.float32(0.0)), axis=1)
    count = 2 * rows_here
    before = jnp.tril(jnp.ones((count, count), jnp.bfloat16), -1)
    rank = jnp.dot(before, named.astype(jnp.bfloat16), preferred_element_type=jnp.float32)
    taken = jnp.logical_and(
        named[:, :, None], rank[:, :, None] == jnp.arange(SLOTS, dtype=jnp.float32)
    )
    combining = jnp.where(taken, row_weight[:, :, None], jnp.float32(0.0)).reshape(count, -1)
    placing = taken.astype(jnp.bfloat16).reshape(count, -1)
    buffer = lax.dot_general(
        placing, rows, (((0,), (0,)), ((), ())), preferred_element_type=jnp.float32
    ).astype(jnp.bfloat16).reshape(PLANE, NY * SLOTS, half)

    landed = by_place(buffer)
    more, sent, at = routes(partner)
    landed, more, sent, at, gate = lax.optimization_barrier((landed, more, sent, at, gate))
    spread_gate = by_place(gate)

    landed = landed.reshape(PLANE, NY, SLOTS, half)
    near = landed[:, 0].reshape(-1, half)
    far = diagonal_chip(landed[:, 1].reshape(-1, half))
    block = near.shape[0]
    mine = (
        jnp.concatenate([near, near_chip(near)]),
        jnp.concatenate([far, near_chip(far)]),
    )
    theirs = tuple(other_core(m) for m in mine)
    spread_gate, mine, theirs, upper = lax.optimization_barrier((spread_gate, mine, theirs, upper))
    spread_up = by_place(upper)

    first_gate = pick(sent[:CAPACITY], spread_gate, CAPACITY)
    got_gate = other_plane(first_gate)
    core = lax.axis_index("core").astype(jnp.int32).reshape(1)
    first_gate, core = after(first_gate, core)
    keep, send = ffn(core, mine, theirs, w_gate[0], w_up[0], w_down[0])
    sent_here = other_core(send)
    spread_up, got_gate, sent_here, down = lax.optimization_barrier(
        (spread_up, got_gate, sent_here, down)
    )
    spread_down = by_place(down)

    got_up = other_plane(pick(sent[:CAPACITY], spread_up, CAPACITY))
    routed_gate = across(more, sent, at, spread_gate, got_gate)
    spread_down, got_up, routed_gate = lax.optimization_barrier(
        (spread_down, got_up, routed_gate)
    )
    moved_gate = by_place(routed_gate)

    got_down = other_plane(pick(sent[:CAPACITY], spread_down, CAPACITY))
    routed_up = across(more, sent, at, spread_up, got_up)
    moved_gate, got_down, routed_up, sent_here = lax.optimization_barrier(
        (moved_gate, got_down, routed_up, sent_here)
    )
    moved_up = by_place(routed_up)

    def part(i):
        rows = slice(i * block, (i + 1) * block)
        return keep[rows] + sent_here[rows].astype(jnp.float32)

    back = near_chip(jnp.concatenate([part(1), part(3)]).astype(jnp.bfloat16))
    back = back.astype(jnp.float32)
    near = (part(0) + back[:block]).astype(jnp.bfloat16)
    far = diagonal_chip((part(2) + back[block:]).astype(jnp.bfloat16))
    total = jnp.stack([p.reshape(PLANE, SLOTS, half) for p in (near, far)], axis=1)
    total = total.reshape(PLANE, NY * SLOTS, half)
    routed_down = across(more, sent, at, spread_down, got_down)
    moved_gate = duplicate(moved_gate)
    moved_up, total, routed_down, moved_gate = lax.optimization_barrier(
        (moved_up, total, routed_down, moved_gate)
    )
    returned = by_place(total).reshape(-1, half)
    returned, routed_down = after(returned, routed_down)
    moved_down = by_place(routed_down)
    moved_up = duplicate(moved_up)

    mixed = jnp.dot(
        combining,
        returned.astype(jnp.float32),
        precision=lax.Precision.HIGHEST,
        preferred_element_type=jnp.float32,
    ).astype(jnp.bfloat16)
    mine = jnp.where(first, mixed[:rows_here], mixed[rows_here:])
    theirs = other_core(jnp.where(first, mixed[rows_here:], mixed[:rows_here]))
    mixed = jnp.where(
        first,
        jnp.concatenate([mine, theirs], axis=1),
        jnp.concatenate([theirs, mine], axis=1),
    )
    moved = (moved_gate, moved_up, moved_down)
    return (mixed,) + tuple(m.reshape(w_gate.shape) for m in moved)


def solution(mesh):
    chips = Mesh(mesh.devices.reshape(2, 2, NZ, NX, NY), ("y_lo", "core", "z", "x", "y_hi"))
    dp, expert = ("y_lo", "core"), ("z", "x", "y_hi")
    rows = P(dp + expert, None)
    weights = P(expert, None, dp)
    return jax.shard_map(
        local,
        mesh=chips,
        in_specs=(rows, rows, rows, P(), weights, weights, weights),
        out_specs=(rows, weights, weights, weights),
        check_vma=False,
    )
```

```python
import jax
import jax.numpy as jnp
from jax import lax
from jax.experimental import pallas as pl
from jax.experimental.pallas import tpu as pltpu
from jax.sharding import Mesh, PartitionSpec as P

NZ, NX, NY = 4, 4, 2
EXPERTS = NZ * NX * NY
PLANE = NZ * NX
SLOTS = 4
CAPACITY, MORE = 8, (2, PLANE - 8)


def other_core(part):
    return lax.ppermute(part, "core", [(0, 1), (1, 0)])


def other_plane(part):
    return lax.ppermute(part, "y_hi", [(0, 1), (1, 0)])


def near_chip(part):
    return lax.ppermute(part, "y_lo", [(0, 1), (1, 0)])


def diagonal_chip(part):
    return lax.ppermute(part, ("y_lo", "y_hi"), [(i, 3 - i) for i in range(4)])


def by_place(part):
    return lax.all_to_all(part, ("x", "z"), split_axis=0, concat_axis=0, tiled=True)


def routes(partner):
    side = lax.axis_index("y_hi")
    place = jnp.arange(PLANE, dtype=jnp.int32)
    expert = (place % NZ) * (NX * NY) + (place // NZ) * NY

    def mates(plane):
        onehot = expert[:, None] + plane == jnp.arange(EXPERTS, dtype=jnp.int32)[None, :]
        return jnp.sum(jnp.where(onehot, partner[None, :], 0), axis=1)

    def crossing_before(crossing):
        earlier = place[None, :] < place[:, None]
        return jnp.sum(jnp.where(earlier, crossing[None, :].astype(jnp.int32), 0), axis=1)

    mine, theirs = mates(side), mates(1 - side)
    crossing = mine % NY != side
    rank = crossing_before(crossing)
    rank_there = crossing_before(theirs % NY == side)
    sent = jnp.sum(
        jnp.where(jnp.logical_and(crossing[None, :], rank[None, :] == place[:, None]), place, 0),
        axis=1,
    )
    source = (mine // NY % NX) * NZ + mine // (NX * NY)
    arrived = jnp.sum(
        jnp.where(source[:, None] == place[None, :], rank_there[None, :], 0), axis=1
    )
    crosses = crossing.astype(jnp.int32)
    where = crosses * (1 + (arrived >= CAPACITY))
    at = jnp.stack(
        [
            jnp.where(crossing, 0, source),
            jnp.where(where == 1, arrived, 0),
            jnp.where(where == 2, arrived - CAPACITY, 0),
            where,
        ]
    )
    count = jnp.sum(crosses)
    level = (count > CAPACITY).astype(jnp.int32) + (count > CAPACITY + MORE[0])
    return level, sent, at


def pick_kernel(at_ref, *refs):
    out = refs[-1]
    for g in range(len(refs) - 1):
        out[g] = refs[g][0]


def pick(at, blocks, count):
    shape = blocks.shape[1:]
    group = count // 2
    size = 2 * count * shape[0] * shape[1]

    def spec(g):
        return pl.BlockSpec((1,) + shape, lambda i, at_ref: (at_ref[i * group + g], 0, 0))

    return pl.pallas_call(
        pick_kernel,
        out_shape=jax.ShapeDtypeStruct((count,) + shape, blocks.dtype),
        grid_spec=pltpu.PrefetchScalarGridSpec(
            num_scalar_prefetch=1,
            grid=(count // group,),
            in_specs=[spec(g) for g in range(group)],
            out_specs=pl.BlockSpec((group,) + shape, lambda i, at_ref: (i, 0, 0)),
        ),
        cost_estimate=pl.CostEstimate(flops=0, bytes_accessed=2 * size, transcendentals=0),
        name="pick",
    )(at, *([blocks] * group))


GROUP = 4


def merge_kernel(at_ref, *refs):
    out = refs[-1]
    for g in range(GROUP):
        where = at_ref[3, pl.program_id(0) * GROUP + g]
        for row in range(3):

            @pl.when(where == row)
            def _():
                out[g] = refs[3 * g + row][0]


def merge(at, sources):
    shape = sources[0].shape[1:]
    size = 2 * PLANE * shape[0] * shape[1]

    def spec(g, row):
        return pl.BlockSpec((1,) + shape, lambda i, at_ref: (at_ref[row, i * GROUP + g], 0, 0))

    return pl.pallas_call(
        merge_kernel,
        out_shape=jax.ShapeDtypeStruct((PLANE,) + shape, sources[0].dtype),
        grid_spec=pltpu.PrefetchScalarGridSpec(
            num_scalar_prefetch=1,
            grid=(PLANE // GROUP,),
            in_specs=[spec(g, row) for g in range(GROUP) for row in range(3)],
            out_specs=pl.BlockSpec((GROUP,) + shape, lambda i, at_ref: (i, 0, 0)),
        ),
        cost_estimate=pl.CostEstimate(flops=0, bytes_accessed=2 * size, transcendentals=0),
        name="merge",
    )(at, *(list(sources) * GROUP))


def extra(more, sent, spread):
    def none(sent, spread):
        return jnp.zeros((MORE[-1],) + spread.shape[1:], spread.dtype)

    def some(count):
        def run(sent, spread):
            late = other_plane(pick(sent[CAPACITY : CAPACITY + count], spread, count))
            return jnp.pad(late, ((0, MORE[-1] - count), (0, 0), (0, 0)))

        return run

    return lax.switch(more, [none] + [some(count) for count in MORE], sent, spread)


def copy_kernel(in_ref, out_ref):
    out_ref[...] = in_ref[...]


def duplicate(value):
    steps = 8
    block = pl.BlockSpec((value.shape[0] // steps,) + value.shape[1:], lambda i: (i, 0, 0))
    return pl.pallas_call(
        copy_kernel,
        out_shape=jax.ShapeDtypeStruct(value.shape, value.dtype),
        grid=(steps,),
        in_specs=[block],
        out_specs=block,
        cost_estimate=pl.CostEstimate(
            flops=0, bytes_accessed=4 * value.size, transcendentals=0
        ),
        name="duplicate",
    )(value)


def after(done, value):
    return lax.optimization_barrier((done, value))


def ffn_kernel(mine_ref, theirs_ref, gate_ref, up_ref, down_ref, keep_ref, send_ref, rows_ref):
    count = mine_ref.shape[0]
    rows_ref[:count, :] = mine_ref[...]
    rows_ref[count:, :] = theirs_ref[...]
    rows = rows_ref[...]
    gate = jnp.dot(rows, gate_ref[...], preferred_element_type=jnp.float32)
    upper = jnp.dot(rows, up_ref[...], preferred_element_type=jnp.float32)
    inner = (gate / (1.0 + jnp.exp(-gate)) * upper).astype(jnp.bfloat16)
    output = lax.dot_general(
        inner, down_ref[...], (((1,), (1,)), ((), ())), preferred_element_type=jnp.float32
    )
    keep_ref[...] = output[:count]
    send_ref[...] = output[count:].astype(jnp.bfloat16)


def ffn(mine, theirs, w_gate, w_up, w_down):
    count, width = mine.shape
    hidden_units = w_gate.shape[1]
    vmem = pl.BlockSpec(memory_space=pltpu.VMEM)
    return pl.pallas_call(
        ffn_kernel,
        out_shape=(
            jax.ShapeDtypeStruct((count, width), jnp.float32),
            jax.ShapeDtypeStruct((count, width), jnp.bfloat16),
        ),
        in_specs=[vmem] * 5,
        out_specs=(vmem, vmem),
        scratch_shapes=[pltpu.VMEM((2 * count, width), jnp.bfloat16)],
        compiler_params=pltpu.CompilerParams(vmem_limit_bytes=48 * 2**20),
        cost_estimate=pl.CostEstimate(
            flops=12 * count * width * hidden_units,
            bytes_accessed=10 * count * width + 6 * width * hidden_units,
            transcendentals=2 * count * hidden_units,
        ),
        name="ffn",
    )(mine, theirs, w_gate, w_up, w_down)


def local(hidden, expert_ids, router_scores, partner, w_gate, w_up, w_down):
    count, width = hidden.shape
    piece = width // PLANE
    hidden_units = w_gate.shape[2]
    gate, upper, down = (w.reshape(PLANE, piece, hidden_units) for w in (w_gate, w_up, w_down))

    side = lax.axis_index("y_hi")
    ids = expert_ids
    relative = (ids // NY % NX * NZ + ids // (NX * NY)) * NY + (ids % NY != side)
    hits = relative[:, :, None] == jnp.arange(EXPERTS, dtype=jnp.int32)
    named = jnp.any(hits, axis=1)
    before = jnp.tril(jnp.ones((count, count), jnp.bfloat16), -1)
    rank = jnp.dot(before, named.astype(jnp.bfloat16), preferred_element_type=jnp.float32)
    taken = jnp.logical_and(
        named[:, :, None], rank[:, :, None] == jnp.arange(SLOTS, dtype=jnp.float32)
    )
    placing = taken.astype(jnp.bfloat16).reshape(count, -1)
    buffer = lax.dot_general(
        placing, hidden, (((0,), (0,)), ((), ())), preferred_element_type=jnp.float32
    )
    buffer = buffer.astype(jnp.bfloat16).reshape(PLANE, NY * SLOTS, width)

    landed = by_place(buffer)
    more, sent, at = routes(partner)
    landed, more, sent, at, gate = lax.optimization_barrier((landed, more, sent, at, gate))
    spread_gate = by_place(gate)

    landed = landed.reshape(PLANE, NY, SLOTS, width)
    near = landed[:, 0].reshape(-1, width)
    far = diagonal_chip(landed[:, 1].reshape(-1, width))
    block = near.shape[0]
    keep, send = [], []
    for rows in (near, far):
        mine = jnp.concatenate([rows, near_chip(rows)])
        kept, other = ffn(mine, other_core(mine), w_gate[0], w_up[0], w_down[0])
        keep.append(kept)
        send.append(other)
    spread_gate, send, upper = lax.optimization_barrier((spread_gate, send, upper))
    spread_up = by_place(upper)

    got_gate = other_plane(pick(sent[:CAPACITY], spread_gate, CAPACITY))
    late_gate = extra(more, sent, spread_gate)
    sent_here = [other_core(s) for s in send]
    spread_up, got_gate, late_gate, sent_here, down = lax.optimization_barrier(
        (spread_up, got_gate, late_gate, sent_here, down)
    )
    spread_down = by_place(down)

    got_up = other_plane(pick(sent[:CAPACITY], spread_up, CAPACITY))
    routed_gate = merge(at, [spread_gate, got_gate, late_gate])
    routed_gate, more = after(routed_gate, more)
    late_up = extra(more, sent, spread_up)
    spread_down, got_up, late_up, routed_gate = lax.optimization_barrier(
        (spread_down, got_up, late_up, routed_gate)
    )
    moved_gate = by_place(routed_gate)

    got_down = other_plane(pick(sent[:CAPACITY], spread_down, CAPACITY))
    routed_up = merge(at, [spread_up, got_up, late_up])
    routed_up, more = after(routed_up, more)
    late_down = extra(more, sent, spread_down)
    part = [kept + here.astype(jnp.float32) for kept, here in zip(keep, sent_here)]
    away = jnp.concatenate([p[block:] for p in part]).astype(jnp.bfloat16)
    home = [p[:block] for p in part]
    moved_gate, got_down, late_down, routed_up, away, home = lax.optimization_barrier(
        (moved_gate, got_down, late_down, routed_up, away, home)
    )
    moved_up = by_place(routed_up)

    back = near_chip(away)
    near, far = (
        (p + b.astype(jnp.float32)).astype(jnp.bfloat16)
        for p, b in zip(home, (back[:block], back[block:]))
    )
    order = jnp.arange(2 * block, dtype=jnp.int32)
    lane = order % (NY * SLOTS)
    source = lane // SLOTS * block + order // (NY * SLOTS) * SLOTS + lane % SLOTS
    shuffle = (source[:, None] == order[None, :]).astype(jnp.bfloat16)
    total = jnp.dot(
        shuffle,
        jnp.concatenate([near, diagonal_chip(far)]),
        preferred_element_type=jnp.float32,
    )
    total = total.astype(jnp.bfloat16).reshape(PLANE, NY * SLOTS, width)
    routed_down = merge(at, [spread_down, got_down, late_down])
    moved_gate = duplicate(moved_gate)
    moved_up, total, routed_down, moved_gate = lax.optimization_barrier(
        (moved_up, total, routed_down, moved_gate)
    )
    returned = by_place(total).reshape(-1, width)
    returned, routed_down = after(returned, routed_down)
    moved_down = by_place(routed_down)
    moved_up = duplicate(moved_up)

    row_weights = router_scores / jnp.sum(router_scores, axis=1, keepdims=True)
    row_weight = jnp.sum(jnp.where(hits, row_weights[:, :, None], jnp.float32(0.0)), axis=1)
    combining = jnp.where(taken, row_weight[:, :, None], jnp.float32(0.0)).reshape(count, -1)
    mixed = jnp.dot(
        combining,
        returned.astype(jnp.float32),
        precision=lax.Precision.HIGHEST,
        preferred_element_type=jnp.float32,
    ).astype(jnp.bfloat16)
    moved = (moved_gate, moved_up, moved_down)
    return (mixed,) + tuple(m.reshape(w_gate.shape) for m in moved)


def solution(mesh):
    chips = Mesh(mesh.devices.reshape(2, 2, NZ, NX, NY), ("y_lo", "core", "z", "x", "y_hi"))
    dp, expert = ("y_lo", "core"), ("z", "x", "y_hi")
    rows = P(dp + expert, None)
    weights = P(expert, None, dp)
    return jax.shard_map(
        local,
        mesh=chips,
        in_specs=(rows, rows, rows, P(), weights, weights, weights),
        out_specs=(rows, weights, weights, weights),
        check_vma=False,
    )
```

```python
import jax
import jax.numpy as jnp
from jax import lax
from jax.experimental import pallas as pl
from jax.experimental.pallas import tpu as pltpu
from jax.sharding import Mesh, PartitionSpec as P

NZ, NX, NY = 4, 4, 2
EXPERTS = NZ * NX * NY
PLANE = NZ * NX
SLOTS = 4
CAPACITY, MORE = 8, (2, 4, PLANE - 8)


def other_core(part):
    return lax.ppermute(part, "core", [(0, 1), (1, 0)])


def other_plane(part):
    return lax.ppermute(part, "y_hi", [(0, 1), (1, 0)])


def near_chip(part):
    return lax.ppermute(part, "y_lo", [(0, 1), (1, 0)])


def diagonal_chip(part):
    return lax.ppermute(part, ("y_lo", "y_hi"), [(i, 3 - i) for i in range(4)])


def by_place(part):
    return lax.all_to_all(part, ("x", "z"), split_axis=0, concat_axis=0, tiled=True)


def routes(partner):
    side = lax.axis_index("y_hi")
    place = jnp.arange(PLANE, dtype=jnp.int32)
    expert = (place % NZ) * (NX * NY) + (place // NZ) * NY

    def mates(plane):
        onehot = expert[:, None] + plane == jnp.arange(EXPERTS, dtype=jnp.int32)[None, :]
        return jnp.sum(jnp.where(onehot, partner[None, :], 0), axis=1)

    def crossing_before(crossing):
        earlier = place[None, :] < place[:, None]
        return jnp.sum(jnp.where(earlier, crossing[None, :].astype(jnp.int32), 0), axis=1)

    mine, theirs = mates(side), mates(1 - side)
    crossing = mine % NY != side
    rank = crossing_before(crossing)
    rank_there = crossing_before(theirs % NY == side)
    sent = jnp.sum(
        jnp.where(jnp.logical_and(crossing[None, :], rank[None, :] == place[:, None]), place, 0),
        axis=1,
    )
    source = (mine // NY % NX) * NZ + mine // (NX * NY)
    arrived = jnp.sum(
        jnp.where(source[:, None] == place[None, :], rank_there[None, :], 0), axis=1
    )
    crosses = crossing.astype(jnp.int32)
    where = crosses * (1 + (arrived >= CAPACITY))
    at = jnp.stack(
        [
            jnp.where(crossing, 0, source),
            jnp.where(where == 1, arrived, 0),
            jnp.where(where == 2, arrived - CAPACITY, 0),
            where,
        ]
    )
    count = jnp.sum(crosses)
    level = sum((count > CAPACITY + m).astype(jnp.int32) for m in (0,) + MORE[:-1])
    return level, sent, at


def pick_kernel(at_ref, *refs):
    out = refs[-1]
    for g in range(len(refs) - 1):
        out[g] = refs[g][0]


def pick(at, blocks, count):
    shape = blocks.shape[1:]
    group = count // 2
    size = 2 * count * shape[0] * shape[1]

    def spec(g):
        return pl.BlockSpec((1,) + shape, lambda i, at_ref: (at_ref[i * group + g], 0, 0))

    return pl.pallas_call(
        pick_kernel,
        out_shape=jax.ShapeDtypeStruct((count,) + shape, blocks.dtype),
        grid_spec=pltpu.PrefetchScalarGridSpec(
            num_scalar_prefetch=1,
            grid=(count // group,),
            in_specs=[spec(g) for g in range(group)],
            out_specs=pl.BlockSpec((group,) + shape, lambda i, at_ref: (i, 0, 0)),
        ),
        cost_estimate=pl.CostEstimate(flops=0, bytes_accessed=2 * size, transcendentals=0),
        name="pick",
    )(at, *([blocks] * group))


GROUP = 4


def merge_kernel(at_ref, *refs):
    out = refs[-1]
    for g in range(GROUP):
        where = at_ref[3, pl.program_id(0) * GROUP + g]
        for row in range(3):

            @pl.when(where == row)
            def _():
                out[g] = refs[3 * g + row][0]


def merge(at, sources):
    shape = sources[0].shape[1:]
    size = 2 * PLANE * shape[0] * shape[1]

    def spec(g, row):
        return pl.BlockSpec((1,) + shape, lambda i, at_ref: (at_ref[row, i * GROUP + g], 0, 0))

    return pl.pallas_call(
        merge_kernel,
        out_shape=jax.ShapeDtypeStruct((PLANE,) + shape, sources[0].dtype),
        grid_spec=pltpu.PrefetchScalarGridSpec(
            num_scalar_prefetch=1,
            grid=(PLANE // GROUP,),
            in_specs=[spec(g, row) for g in range(GROUP) for row in range(3)],
            out_specs=pl.BlockSpec((GROUP,) + shape, lambda i, at_ref: (i, 0, 0)),
        ),
        cost_estimate=pl.CostEstimate(flops=0, bytes_accessed=2 * size, transcendentals=0),
        name="merge",
    )(at, *(list(sources) * GROUP))


def extra(more, sent, spread):
    def none(sent, spread):
        return jnp.zeros((MORE[-1],) + spread.shape[1:], spread.dtype)

    def some(count):
        def run(sent, spread):
            late = other_plane(pick(sent[CAPACITY : CAPACITY + count], spread, count))
            return jnp.pad(late, ((0, MORE[-1] - count), (0, 0), (0, 0)))

        return run

    return lax.switch(more, [none] + [some(count) for count in MORE], sent, spread)


def copy_kernel(in_ref, out_ref):
    out_ref[...] = in_ref[...]


def duplicate(value):
    steps = 8
    block = pl.BlockSpec((value.shape[0] // steps,) + value.shape[1:], lambda i: (i, 0, 0))
    return pl.pallas_call(
        copy_kernel,
        out_shape=jax.ShapeDtypeStruct(value.shape, value.dtype),
        grid=(steps,),
        in_specs=[block],
        out_specs=block,
        cost_estimate=pl.CostEstimate(
            flops=0, bytes_accessed=4 * value.size, transcendentals=0
        ),
        name="duplicate",
    )(value)


def after(done, value):
    return lax.optimization_barrier((done, value))


def ffn_kernel(mine_ref, theirs_ref, gate_ref, up_ref, down_ref, keep_ref, send_ref, rows_ref):
    count = mine_ref.shape[0]
    rows_ref[:count, :] = mine_ref[...]
    rows_ref[count:, :] = theirs_ref[...]
    rows = rows_ref[...]
    gate = jnp.dot(rows, gate_ref[...], preferred_element_type=jnp.float32)
    upper = jnp.dot(rows, up_ref[...], preferred_element_type=jnp.float32)
    inner = (gate / (1.0 + jnp.exp(-gate)) * upper).astype(jnp.bfloat16)
    output = lax.dot_general(
        inner, down_ref[...], (((1,), (1,)), ((), ())), preferred_element_type=jnp.float32
    )
    keep_ref[...] = output[:count]
    send_ref[...] = output[count:].astype(jnp.bfloat16)


def ffn(mine, theirs, w_gate, w_up, w_down):
    count, width = mine.shape
    hidden_units = w_gate.shape[1]
    vmem = pl.BlockSpec(memory_space=pltpu.VMEM)
    return pl.pallas_call(
        ffn_kernel,
        out_shape=(
            jax.ShapeDtypeStruct((count, width), jnp.float32),
            jax.ShapeDtypeStruct((count, width), jnp.bfloat16),
        ),
        in_specs=[vmem] * 5,
        out_specs=(vmem, vmem),
        scratch_shapes=[pltpu.VMEM((2 * count, width), jnp.bfloat16)],
        compiler_params=pltpu.CompilerParams(vmem_limit_bytes=48 * 2**20),
        cost_estimate=pl.CostEstimate(
            flops=12 * count * width * hidden_units,
            bytes_accessed=10 * count * width + 6 * width * hidden_units,
            transcendentals=2 * count * hidden_units,
        ),
        name="ffn",
    )(mine, theirs, w_gate, w_up, w_down)


def local(hidden, expert_ids, router_scores, partner, w_gate, w_up, w_down):
    count, width = hidden.shape
    piece = width // PLANE
    hidden_units = w_gate.shape[2]
    gate, upper, down = (w.reshape(PLANE, piece, hidden_units) for w in (w_gate, w_up, w_down))

    side = lax.axis_index("y_hi")
    ids = expert_ids
    relative = (ids // NY % NX * NZ + ids // (NX * NY)) * NY + (ids % NY != side)
    hits = relative[:, :, None] == jnp.arange(EXPERTS, dtype=jnp.int32)
    named = jnp.any(hits, axis=1)
    before = jnp.tril(jnp.ones((count, count), jnp.bfloat16), -1)
    rank = jnp.dot(before, named.astype(jnp.bfloat16), preferred_element_type=jnp.float32)
    taken = jnp.logical_and(
        named[:, :, None], rank[:, :, None] == jnp.arange(SLOTS, dtype=jnp.float32)
    )
    placing = taken.astype(jnp.bfloat16).reshape(count, -1)
    buffer = lax.dot_general(
        placing, hidden, (((0,), (0,)), ((), ())), preferred_element_type=jnp.float32
    )
    buffer = buffer.astype(jnp.bfloat16).reshape(PLANE, NY * SLOTS, width)

    landed = by_place(buffer)
    more, sent, at = routes(partner)
    landed, more, sent, at, gate = lax.optimization_barrier((landed, more, sent, at, gate))
    spread_gate = by_place(gate)

    landed = landed.reshape(-1, width)
    block = PLANE * SLOTS
    order = jnp.arange(block, dtype=jnp.int32)
    wanted = order // SLOTS * NY * SLOTS + order % SLOTS
    held = jnp.arange(2 * block, dtype=jnp.int32)

    def rows_of(plane):
        choice = (wanted[:, None] + plane * SLOTS == held[None, :]).astype(jnp.bfloat16)
        rows = jnp.dot(choice, landed, preferred_element_type=jnp.float32)
        return rows.astype(jnp.bfloat16)

    near, far = rows_of(0), diagonal_chip(rows_of(1))
    keep, send = [], []
    for rows in (near, far):
        mine = jnp.concatenate([rows, near_chip(rows)])
        kept, other = ffn(mine, other_core(mine), w_gate[0], w_up[0], w_down[0])
        keep.append(kept)
        send.append(other)
    spread_gate, send, upper = lax.optimization_barrier((spread_gate, send, upper))
    spread_up = by_place(upper)

    got_gate = other_plane(pick(sent[:CAPACITY], spread_gate, CAPACITY))
    late_gate = extra(more, sent, spread_gate)
    sent_here = [other_core(s) for s in send]
    spread_up, got_gate, late_gate, sent_here, down = lax.optimization_barrier(
        (spread_up, got_gate, late_gate, sent_here, down)
    )
    spread_down = by_place(down)

    got_up = other_plane(pick(sent[:CAPACITY], spread_up, CAPACITY))
    routed_gate = merge(at, [spread_gate, got_gate, late_gate])
    routed_gate, more = after(routed_gate, more)
    late_up = extra(more, sent, spread_up)
    spread_down, got_up, late_up, routed_gate = lax.optimization_barrier(
        (spread_down, got_up, late_up, routed_gate)
    )
    moved_gate = by_place(routed_gate)

    got_down = other_plane(pick(sent[:CAPACITY], spread_down, CAPACITY))
    routed_up = merge(at, [spread_up, got_up, late_up])
    routed_up, more = after(routed_up, more)
    late_down = extra(more, sent, spread_down)
    part = [kept + here.astype(jnp.float32) for kept, here in zip(keep, sent_here)]
    away = jnp.concatenate([p[block:] for p in part]).astype(jnp.bfloat16)
    home = [p[:block] for p in part]
    moved_gate, got_down, late_down, routed_up, away, home = lax.optimization_barrier(
        (moved_gate, got_down, late_down, routed_up, away, home)
    )
    moved_up = by_place(routed_up)

    back = near_chip(away)
    near, far = (
        (p + b.astype(jnp.float32)).astype(jnp.bfloat16)
        for p, b in zip(home, (back[:block], back[block:]))
    )
    order = jnp.arange(2 * block, dtype=jnp.int32)
    lane = order % (NY * SLOTS)
    source = lane // SLOTS * block + order // (NY * SLOTS) * SLOTS + lane % SLOTS
    shuffle = (source[:, None] == order[None, :]).astype(jnp.bfloat16)
    total = jnp.dot(
        shuffle,
        jnp.concatenate([near, diagonal_chip(far)]),
        preferred_element_type=jnp.float32,
    )
    total = total.astype(jnp.bfloat16).reshape(PLANE, NY * SLOTS, width)
    routed_down = merge(at, [spread_down, got_down, late_down])
    moved_gate = duplicate(moved_gate)
    moved_up, total, routed_down, moved_gate = lax.optimization_barrier(
        (moved_up, total, routed_down, moved_gate)
    )
    returned = by_place(total).reshape(-1, width)
    returned, routed_down = after(returned, routed_down)
    moved_down = by_place(routed_down)
    moved_up = duplicate(moved_up)

    row_weights = router_scores / jnp.sum(router_scores, axis=1, keepdims=True)
    row_weight = jnp.sum(jnp.where(hits, row_weights[:, :, None], jnp.float32(0.0)), axis=1)
    combining = jnp.where(taken, row_weight[:, :, None], jnp.float32(0.0)).reshape(count, -1)
    mixed = jnp.dot(
        combining,
        returned.astype(jnp.float32),
        precision=lax.Precision.HIGHEST,
        preferred_element_type=jnp.float32,
    ).astype(jnp.bfloat16)
    moved = (moved_gate, moved_up, moved_down)
    return (mixed,) + tuple(m.reshape(w_gate.shape) for m in moved)


def solution(mesh):
    chips = Mesh(mesh.devices.reshape(2, 2, NZ, NX, NY), ("y_lo", "core", "z", "x", "y_hi"))
    dp, expert = ("y_lo", "core"), ("z", "x", "y_hi")
    rows = P(dp + expert, None)
    weights = P(expert, None, dp)
    return jax.shard_map(
        local,
        mesh=chips,
        in_specs=(rows, rows, rows, P(), weights, weights, weights),
        out_specs=(rows, weights, weights, weights),
        check_vma=False,
    )
```

```python
import jax
import jax.numpy as jnp
from jax import lax
from jax.experimental import pallas as pl
from jax.experimental.pallas import tpu as pltpu
from jax.sharding import Mesh, PartitionSpec as P

NZ, NX, NY = 4, 4, 2
EXPERTS = NZ * NX * NY
PLANE = NZ * NX
SLOTS = 4
CAPACITY, MORE = 8, (2, 4, PLANE - 8)


def other_core(part):
    return lax.ppermute(part, "core", [(0, 1), (1, 0)])


def other_plane(part):
    return lax.ppermute(part, "y_hi", [(0, 1), (1, 0)])


def near_chip(part):
    return lax.ppermute(part, "y_lo", [(0, 1), (1, 0)])


def diagonal_chip(part):
    return lax.ppermute(part, ("y_lo", "y_hi"), [(i, 3 - i) for i in range(4)])


def by_place(part):
    return lax.all_to_all(part, ("x", "z"), split_axis=0, concat_axis=0, tiled=True)


def routes(partner):
    side = lax.axis_index("y_hi")
    place = jnp.arange(PLANE, dtype=jnp.int32)
    expert = (place % NZ) * (NX * NY) + (place // NZ) * NY

    def mates(plane):
        onehot = expert[:, None] + plane == jnp.arange(EXPERTS, dtype=jnp.int32)[None, :]
        return jnp.sum(jnp.where(onehot, partner[None, :], 0), axis=1)

    def crossing_before(crossing):
        earlier = place[None, :] < place[:, None]
        return jnp.sum(jnp.where(earlier, crossing[None, :].astype(jnp.int32), 0), axis=1)

    mine, theirs = mates(side), mates(1 - side)
    crossing = mine % NY != side
    rank = crossing_before(crossing)
    rank_there = crossing_before(theirs % NY == side)
    sent = jnp.sum(
        jnp.where(jnp.logical_and(crossing[None, :], rank[None, :] == place[:, None]), place, 0),
        axis=1,
    )
    source = (mine // NY % NX) * NZ + mine // (NX * NY)
    arrived = jnp.sum(
        jnp.where(source[:, None] == place[None, :], rank_there[None, :], 0), axis=1
    )
    crosses = crossing.astype(jnp.int32)
    where = crosses * (1 + (arrived >= CAPACITY))
    at = jnp.stack(
        [
            jnp.where(crossing, 0, source),
            jnp.where(where == 1, arrived, 0),
            jnp.where(where == 2, arrived - CAPACITY, 0),
            where,
        ]
    )
    count = jnp.sum(crosses)
    level = sum((count > CAPACITY + m).astype(jnp.int32) for m in (0,) + MORE[:-1])
    return level, sent, at


def pick_kernel(at_ref, *refs):
    out = refs[-1]
    for g in range(len(refs) - 1):
        out[g] = refs[g][0]


def pick(at, blocks, count):
    shape = blocks.shape[1:]
    group = count // 2
    size = 2 * count * shape[0] * shape[1]

    def spec(g):
        return pl.BlockSpec((1,) + shape, lambda i, at_ref: (at_ref[i * group + g], 0, 0))

    return pl.pallas_call(
        pick_kernel,
        out_shape=jax.ShapeDtypeStruct((count,) + shape, blocks.dtype),
        grid_spec=pltpu.PrefetchScalarGridSpec(
            num_scalar_prefetch=1,
            grid=(count // group,),
            in_specs=[spec(g) for g in range(group)],
            out_specs=pl.BlockSpec((group,) + shape, lambda i, at_ref: (i, 0, 0)),
        ),
        cost_estimate=pl.CostEstimate(flops=0, bytes_accessed=2 * size, transcendentals=0),
        name="pick",
    )(at, *([blocks] * group))


GROUP = 4


def merge_kernel(at_ref, *refs):
    out = refs[-1]
    for g in range(GROUP):
        where = at_ref[3, pl.program_id(0) * GROUP + g]
        for row in range(3):

            @pl.when(where == row)
            def _():
                out[g] = refs[3 * g + row][0]


def merge(at, sources):
    shape = sources[0].shape[1:]
    size = 2 * PLANE * shape[0] * shape[1]

    def spec(g, row):
        return pl.BlockSpec((1,) + shape, lambda i, at_ref: (at_ref[row, i * GROUP + g], 0, 0))

    return pl.pallas_call(
        merge_kernel,
        out_shape=jax.ShapeDtypeStruct((PLANE,) + shape, sources[0].dtype),
        grid_spec=pltpu.PrefetchScalarGridSpec(
            num_scalar_prefetch=1,
            grid=(PLANE // GROUP,),
            in_specs=[spec(g, row) for g in range(GROUP) for row in range(3)],
            out_specs=pl.BlockSpec((GROUP,) + shape, lambda i, at_ref: (i, 0, 0)),
        ),
        cost_estimate=pl.CostEstimate(flops=0, bytes_accessed=2 * size, transcendentals=0),
        name="merge",
    )(at, *(list(sources) * GROUP))


def extra(more, sent, spread):
    def none(sent, spread):
        return jnp.zeros((MORE[-1],) + spread.shape[1:], spread.dtype)

    def some(count):
        def run(sent, spread):
            late = other_plane(pick(sent[CAPACITY : CAPACITY + count], spread, count))
            return jnp.pad(late, ((0, MORE[-1] - count), (0, 0), (0, 0)))

        return run

    return lax.switch(more, [none] + [some(count) for count in MORE], sent, spread)


def copy_kernel(in_ref, out_ref):
    out_ref[...] = in_ref[...]


def duplicate(value):
    steps = 8
    block = pl.BlockSpec((value.shape[0] // steps,) + value.shape[1:], lambda i: (i, 0, 0))
    return pl.pallas_call(
        copy_kernel,
        out_shape=jax.ShapeDtypeStruct(value.shape, value.dtype),
        grid=(steps,),
        in_specs=[block],
        out_specs=block,
        cost_estimate=pl.CostEstimate(
            flops=0, bytes_accessed=4 * value.size, transcendentals=0
        ),
        name="duplicate",
    )(value)


def after(done, value):
    return lax.optimization_barrier((done, value))


def ffn_kernel(mine_ref, theirs_ref, gate_ref, up_ref, down_ref, keep_ref, send_ref, rows_ref):
    count = mine_ref.shape[0]
    rows_ref[:count, :] = mine_ref[...]
    rows_ref[count:, :] = theirs_ref[...]
    rows = rows_ref[...]
    gate = jnp.dot(rows, gate_ref[...], preferred_element_type=jnp.float32)
    upper = jnp.dot(rows, up_ref[...], preferred_element_type=jnp.float32)
    inner = (gate / (1.0 + jnp.exp(-gate)) * upper).astype(jnp.bfloat16)
    output = lax.dot_general(
        inner, down_ref[...], (((1,), (1,)), ((), ())), preferred_element_type=jnp.float32
    )
    keep_ref[...] = output[:count]
    send_ref[...] = output[count:].astype(jnp.bfloat16)


def ffn(mine, theirs, w_gate, w_up, w_down):
    count, width = mine.shape
    hidden_units = w_gate.shape[1]
    vmem = pl.BlockSpec(memory_space=pltpu.VMEM)
    return pl.pallas_call(
        ffn_kernel,
        out_shape=(
            jax.ShapeDtypeStruct((count, width), jnp.float32),
            jax.ShapeDtypeStruct((count, width), jnp.bfloat16),
        ),
        in_specs=[vmem] * 5,
        out_specs=(vmem, vmem),
        scratch_shapes=[pltpu.VMEM((2 * count, width), jnp.bfloat16)],
        compiler_params=pltpu.CompilerParams(vmem_limit_bytes=48 * 2**20),
        cost_estimate=pl.CostEstimate(
            flops=12 * count * width * hidden_units,
            bytes_accessed=10 * count * width + 6 * width * hidden_units,
            transcendentals=2 * count * hidden_units,
        ),
        name="ffn",
    )(mine, theirs, w_gate, w_up, w_down)


def local(hidden, expert_ids, router_scores, partner, w_gate, w_up, w_down):
    count, width = hidden.shape
    piece = width // PLANE
    hidden_units = w_gate.shape[2]
    gate, upper, down = (w.reshape(PLANE, piece, hidden_units) for w in (w_gate, w_up, w_down))

    side = lax.axis_index("y_hi")
    ids = expert_ids
    relative = (ids // NY % NX * NZ + ids // (NX * NY)) * NY + (ids % NY != side)
    hits = relative[:, :, None] == jnp.arange(EXPERTS, dtype=jnp.int32)
    named = jnp.any(hits, axis=1)
    before = jnp.tril(jnp.ones((count, count), jnp.bfloat16), -1)
    rank = jnp.dot(before, named.astype(jnp.bfloat16), preferred_element_type=jnp.float32)
    taken = jnp.logical_and(
        named[:, :, None], rank[:, :, None] == jnp.arange(SLOTS, dtype=jnp.float32)
    )
    placing = taken.astype(jnp.bfloat16).reshape(count, -1)
    buffer = lax.dot_general(
        placing, hidden, (((0,), (0,)), ((), ())), preferred_element_type=jnp.float32
    )
    buffer = buffer.astype(jnp.bfloat16).reshape(PLANE, NY * SLOTS, width)

    landed = by_place(buffer)
    more, sent, at = routes(partner)
    landed, more, sent, at, gate = lax.optimization_barrier((landed, more, sent, at, gate))
    spread_gate = by_place(gate)

    landed = landed.reshape(-1, width)
    block = PLANE * SLOTS
    order = jnp.arange(block, dtype=jnp.int32)
    wanted = order // SLOTS * NY * SLOTS + order % SLOTS
    held = jnp.arange(2 * block, dtype=jnp.int32)

    def rows_of(plane):
        choice = (wanted[:, None] + plane * SLOTS == held[None, :]).astype(jnp.bfloat16)
        rows = jnp.dot(choice, landed, preferred_element_type=jnp.float32)
        return rows.astype(jnp.bfloat16)

    near, far = rows_of(0), diagonal_chip(rows_of(1))
    keep, send = [], []
    for rows in (near, far):
        mine = jnp.concatenate([rows, near_chip(rows)])
        kept, other = ffn(mine, other_core(mine), w_gate[0], w_up[0], w_down[0])
        keep.append(kept)
        send.append(other)
    spread_gate, send, upper = lax.optimization_barrier((spread_gate, send, upper))
    spread_up = by_place(upper)

    got_gate = other_plane(pick(sent[:CAPACITY], spread_gate, CAPACITY))
    late_gate = extra(more, sent, spread_gate)
    sent_here = [other_core(s) for s in send]
    spread_up, got_gate, late_gate, sent_here, down = lax.optimization_barrier(
        (spread_up, got_gate, late_gate, sent_here, down)
    )
    spread_down = by_place(down)

    got_up = other_plane(pick(sent[:CAPACITY], spread_up, CAPACITY))
    routed_gate = merge(at, [spread_gate, got_gate, late_gate])
    routed_gate, more = after(routed_gate, more)
    late_up = extra(more, sent, spread_up)
    spread_down, got_up, late_up, routed_gate = lax.optimization_barrier(
        (spread_down, got_up, late_up, routed_gate)
    )
    moved_gate = by_place(routed_gate)

    got_down = other_plane(pick(sent[:CAPACITY], spread_down, CAPACITY))
    routed_up = merge(at, [spread_up, got_up, late_up])
    routed_up, more = after(routed_up, more)
    late_down = extra(more, sent, spread_down)
    part = [kept + here.astype(jnp.float32) for kept, here in zip(keep, sent_here)]
    away = jnp.concatenate([p[block:] for p in part]).astype(jnp.bfloat16)
    home = [p[:block] for p in part]
    moved_gate, got_down, late_down, routed_up, away, home = lax.optimization_barrier(
        (moved_gate, got_down, late_down, routed_up, away, home)
    )
    moved_up = by_place(routed_up)

    back = near_chip(away)
    near, far = (
        (p + b.astype(jnp.float32)).astype(jnp.bfloat16)
        for p, b in zip(home, (back[:block], back[block:]))
    )
    order = jnp.arange(2 * block, dtype=jnp.int32)
    lane = order % (NY * SLOTS)
    source = lane // SLOTS * block + order // (NY * SLOTS) * SLOTS + lane % SLOTS
    shuffle = (source[:, None] == order[None, :]).astype(jnp.bfloat16)
    total = jnp.dot(
        shuffle,
        jnp.concatenate([near, diagonal_chip(far)]),
        preferred_element_type=jnp.float32,
    )
    total = total.astype(jnp.bfloat16).reshape(PLANE, NY * SLOTS, width)
    routed_down = merge(at, [spread_down, got_down, late_down])
    moved_gate = duplicate(moved_gate)
    moved_up, total, routed_down, moved_gate = lax.optimization_barrier(
        (moved_up, total, routed_down, moved_gate)
    )
    moved_down = by_place(routed_down)
    moved_up = duplicate(moved_up)
    moved_down, total, moved_up = lax.optimization_barrier((moved_down, total, moved_up))
    returned = by_place(total).reshape(-1, width)
    moved_down = duplicate(moved_down)

    row_weights = router_scores / jnp.sum(router_scores, axis=1, keepdims=True)
    row_weight = jnp.sum(jnp.where(hits, row_weights[:, :, None], jnp.float32(0.0)), axis=1)
    combining = jnp.where(taken, row_weight[:, :, None], jnp.float32(0.0)).reshape(count, -1)
    mixed = jnp.dot(
        combining,
        returned.astype(jnp.float32),
        precision=lax.Precision.HIGHEST,
        preferred_element_type=jnp.float32,
    ).astype(jnp.bfloat16)
    moved = (moved_gate, moved_up, moved_down)
    return (mixed,) + tuple(m.reshape(w_gate.shape) for m in moved)


def solution(mesh):
    chips = Mesh(mesh.devices.reshape(2, 2, NZ, NX, NY), ("y_lo", "core", "z", "x", "y_hi"))
    dp, expert = ("y_lo", "core"), ("z", "x", "y_hi")
    rows = P(dp + expert, None)
    weights = P(expert, None, dp)
    return jax.shard_map(
        local,
        mesh=chips,
        in_specs=(rows, rows, rows, P(), weights, weights, weights),
        out_specs=(rows, weights, weights, weights),
        check_vma=False,
    )
```
